32 devices in a mesh: dp: 8 (over z, y), tensor: 4 (over x, core).
Axes of the slice: x: 2, y: 2, z: 4, core: 2. Of those that a mesh axis runs over, the one named last changes fastest.
Arguments:
- frames_in: bfloat16 [12000, 1536], P(('dp', 'tensor')), may hold values from -6 to 6
- text_states: bfloat16 [512, 1536], P('dp'), may hold values from -6 to 6
- adapter_pick: int32 [8], P('dp'), may hold values from 0 to 7
- out_grad: bfloat16 [12000, 1536], P('dp'), may hold values from -6 to 6
- norm_gain: float32 [3, 1536], replicated, may hold values from 0.1 to 1.9
- norm_bias: float32 [3, 1536], replicated, may hold values from -3 to 3
- col_w: bfloat16 [6, 1536, 1536], P(None, None, 'tensor'), may hold values from -0.15625 to 0.15625
- col_a: bfloat16 [6, 8, 1536, 16], replicated, may hold values from -0.15625 to 0.15625
- col_b: bfloat16 [6, 8, 16, 1536], P(None, None, None, 'tensor'), may hold values from -1.5 to 1.5
- row_w: bfloat16 [2, 1536, 1536], P(None, 'tensor'), may hold values from -0.625 to 0.625
- row_a: bfloat16 [2, 8, 1536, 16], P(None, None, 'tensor'), may hold values from -0.625 to 0.625
- row_b: bfloat16 [2, 8, 16, 1536], replicated, may hold values from -1.5 to 1.5
- mlp_in: bfloat16 [1536, 6144], P(None, 'tensor'), may hold values from -0.15625 to 0.15625
- mlp_in_a: bfloat16 [8, 1536, 16], replicated, may hold values from -0.15625 to 0.15625
- mlp_in_b: bfloat16 [8, 16, 6144], P(None, None, 'tensor'), may hold values from -1.5 to 1.5
- mlp_out: bfloat16 [6144, 1536], P('tensor'), may hold values from -0.078125 to 0.078125
- mlp_out_a: bfloat16 [8, 6144, 16], P(None, 'tensor'), may hold values from -0.078125 to 0.078125
- mlp_out_b: bfloat16 [8, 16, 1536], replicated, may hold values from -1.5 to 1.5
Outputs:
- block_out: bfloat16 [12000, 1536], P(('dp', 'tensor'))
- frames_grad: float32 [12000, 1536], P(('dp', 'tensor'))
- text_grad: float32 [512, 1536], P(('dp', 'tensor'))
- col_a_grad: float32 [6, 8, 1536, 16], replicated
- col_b_grad: float32 [6, 8, 16, 1536], P(None, None, None, 'tensor')
- row_a_grad: float32 [2, 8, 1536, 16], P(None, None, 'tensor')
- row_b_grad: float32 [2, 8, 16, 1536], replicated
- mlp_in_a_grad: float32 [8, 1536, 16], replicated
- mlp_in_b_grad: float32 [8, 16, 6144], P(None, None, 'tensor')
- mlp_out_a_grad: float32 [8, 6144, 16], P(None, 'tensor')
- mlp_out_b_grad: float32 [8, 16, 1536], replicated
The draws below stay inside these ranges and needn't reach their ends.
All inputs are finite; a program needn't handle non-finite values.
Results may differ from the reference program's by a relative error of at most 0.034.
Values may be sent and summed in bfloat16 or wider, within the bound.
A program may use at most 256 MiB of HBM per device.

```python
import jax
import jax.numpy as jnp
from jax import lax

D = 1536
HEAD = 64
FF = 6144
ADAPTERS = 8
R = 16
FRAMES = 1500
TEXT = 64
CLIPS = 8
ROWS = 12000


def with_ends(array, key, smallest, largest):
    dims = array.shape
    index_at = [jax.random.randint(jax.random.fold_in(key, axis), (), 0, dims[axis]) for axis in range(len(dims))]
    array = array.at[tuple(index_at)].set(smallest)
    longest = dims.index(max(dims))
    index_at[longest] = (index_at[longest] + 1) % dims[longest]
    return array.at[tuple(index_at)].set(largest)


def levels(stream_key, shape, cuts, smallest, largest):
    level = 1.0
    for dim, blocks in cuts:
        heights = jax.random.uniform(jax.random.fold_in(jax.random.fold_in(stream_key, 6), dim), (blocks,), jnp.float32, smallest / len(cuts), largest / len(cuts))
        level = level * jnp.repeat(jnp.exp(heights), shape[dim] // blocks).reshape((-1,) + (1,) * (len(shape) - 1 - dim))
    return level


def bell_draw(rng, shape, deviation, most, cuts=(), kind=jnp.bfloat16):
    factor_of = levels(rng, shape, cuts, -0.22, 0.18) if cuts else 1.0
    values = jax.random.normal(rng, shape, jnp.float32) * deviation * factor_of
    return jnp.minimum(jnp.maximum(values, -most), most).astype(kind)


def setup_inputs(seed: int = 0) -> dict:
    key_list = jax.random.split(jax.random.key(seed), 19)
    return {
        "frames_in": bell_draw(key_list[0], (ROWS, D), 1.0, 6.0, ((0, 32),)),
        "text_states": bell_draw(key_list[1], (CLIPS * TEXT, D), 1.0, 6.0, ((0, 8),)),
        "adapter_pick": with_ends(jax.random.randint(key_list[2], (CLIPS,), 0, ADAPTERS), jax.random.fold_in(key_list[2], 1), 0, ADAPTERS - 1).astype(jnp.int32),
        "out_grad": bell_draw(key_list[3], (ROWS, D), 1.0, 6.0, ((0, 8),)),
        "norm_gain": jnp.clip(1.0 + 0.18 * jax.random.normal(key_list[4], (3, D), jnp.float32), 0.1, 1.9),
        "norm_bias": bell_draw(key_list[5], (3, D), 0.5, 3.0, (), jnp.float32),
        "col_w": bell_draw(key_list[6], (6, D, D), D ** -0.5, 0.15625, ((2, 4),)),
        "col_a": bell_draw(key_list[7], (6, ADAPTERS, D, R), D ** -0.5, 0.15625),
        "col_b": bell_draw(key_list[8], (6, ADAPTERS, R, D), R ** -0.5, 1.5, ((3, 4),)),
        "row_w": bell_draw(key_list[9], (2, D, D), (D // 16) ** -0.5, 0.625, ((1, 4),)),
        "row_a": bell_draw(key_list[10], (2, ADAPTERS, D, R), (D // 16) ** -0.5, 0.625, ((2, 4),)),
        "row_b": bell_draw(key_list[11], (2, ADAPTERS, R, D), R ** -0.5, 1.5),
        "mlp_in": bell_draw(key_list[12], (D, FF), D ** -0.5, 0.15625, ((1, 4),)),
        "mlp_in_a": bell_draw(key_list[13], (ADAPTERS, D, R), D ** -0.5, 0.15625),
        "mlp_in_b": bell_draw(key_list[14], (ADAPTERS, R, FF), R ** -0.5, 1.5, ((2, 4),)),
        "mlp_out": bell_draw(key_list[15], (FF, D), FF ** -0.5, 0.078125, ((0, 4),)),
        "mlp_out_a": bell_draw(key_list[16], (ADAPTERS, FF, R), FF ** -0.5, 0.078125, ((1, 4),)),
        "mlp_out_b": bell_draw(key_list[17], (ADAPTERS, R, D), R ** -0.5, 1.5),
    }


HIGHEST_PRECISION = lax.Precision.HIGHEST
EPSILON = 1e-05

@jax.custom_vjp
def low(v):
    return lax.optimization_barrier(v.astype(jnp.bfloat16)).astype(jnp.float32)

@jax.custom_vjp
def low_back(v):
    return v

def low_keep(v):
    return (low(v), None)

def low_pass(kept, grad):
    return (grad,)

def back_keep(v):
    return (v, None)

def back_low(kept, grad):
    return (low(grad),)
low.defvjp(low_keep, low_pass)
low_back.defvjp(back_keep, back_low)

def matmul(former, latter):
    return jnp.dot(former, latter, precision=HIGHEST_PRECISION)

def normed(values_in, scale_vec, shift_vec):
    row_mean = lax.optimization_barrier(jnp.mean(values_in, axis=-1, keepdims=True))
    centred = values_in - row_mean
    variance = lax.optimization_barrier(jnp.mean(centred * centred, axis=-1, keepdims=True))
    return centred * lax.rsqrt(variance + EPSILON) * scale_vec + shift_vec

def adapted(source, weight, down_map, up_map):
    return matmul(source, weight) + matmul(matmul(source, down_map), up_map)

def attend(queries, first_row, all_keys, all_values):
    scores = low_back(jnp.einsum('qhe,khe->hqk', queries, all_keys, precision=HIGHEST_PRECISION) * 0.125)
    query_pos = first_row + jnp.arange(queries.shape[0], dtype=jnp.int32)
    key_pos = jnp.arange(all_keys.shape[0], dtype=jnp.int32)
    allowed = key_pos[None, None, :] <= query_pos[None, :, None]
    scores = jnp.where(allowed, scores, -1e+30)
    attn_probs = jax.nn.softmax(scores, axis=-1)
    return jnp.einsum('hqk,khe->qhe', low(attn_probs), all_values, precision=HIGHEST_PRECISION)

def clip_layer(clip_rows, clip_text, adapter_index, norm_gain, norm_bias, weights, adapters):
    col_w, row_w, mlp_in, mlp_out = weights
    col_a, col_b, row_a, row_b, mlp_in_a, mlp_in_b, mlp_out_a, mlp_out_b = adapters

    def chosen(stacked, slot_axis):
        return lax.dynamic_index_in_dim(stacked, adapter_index, slot_axis, keepdims=False)
    col_down = chosen(col_a, 1)
    col_up = chosen(col_b, 1)
    row_down = chosen(row_a, 1)
    row_up = chosen(row_b, 1)
    in_down = chosen(mlp_in_a, 0)
    in_up = chosen(mlp_in_b, 0)
    out_down = chosen(mlp_out_a, 0)
    out_up = chosen(mlp_out_b, 0)
    head_count = D // HEAD

    def project(source, proj_slot):
        result = low(low_back(adapted(source, col_w[proj_slot], col_down[proj_slot], col_up[proj_slot])))
        return result.reshape(source.shape[0], head_count, HEAD)
    norm_one = low(normed(clip_rows, norm_gain[0], norm_bias[0]))
    queries = project(norm_one, 0)
    all_keys = project(norm_one, 1)
    all_values = project(norm_one, 2)
    block_count = max(1, FRAMES // 512)
    block_rows = FRAMES // block_count
    starts = jnp.arange(block_count, dtype=jnp.int32) * block_rows
    attend_saved = jax.checkpoint(attend)

    def one_block(pieces):
        return attend_saved(pieces[0], pieces[1], all_keys, all_values)
    attn_mixed = lax.map(one_block, (queries.reshape(block_count, block_rows, head_count, HEAD), starts))
    attended = low(low_back(attn_mixed.reshape(FRAMES, D)))
    first = clip_rows + low_back(adapted(attended, row_w[0], row_down[0], row_up[0]))
    norm_two = low(normed(first, norm_gain[1], norm_bias[1]))
    cross_queries = project(norm_two, 3)
    cross_keys = project(clip_text, 4)
    cross_values = project(clip_text, 5)
    cross_scores = low_back(jnp.einsum('qhe,khe->hqk', cross_queries, cross_keys, precision=HIGHEST_PRECISION) * 0.125)
    cross_probs = jax.nn.softmax(cross_scores, axis=-1)
    cross_mixed = jnp.einsum('hqk,khe->qhe', low(cross_probs), cross_values, precision=HIGHEST_PRECISION)
    cross_mixed = low(low_back(cross_mixed.reshape(FRAMES, D)))
    second = first + low_back(adapted(cross_mixed, row_w[1], row_down[1], row_up[1]))
    norm_three = low(normed(second, norm_gain[2], norm_bias[2]))
    pre = low_back(adapted(norm_three, mlp_in, in_down, in_up))
    hidden = low(jax.nn.gelu(pre, approximate=False))
    return second + low_back(adapted(hidden, mlp_out, out_down, out_up))

def reference(frames_in, text_states, adapter_pick, out_grad, norm_gain, norm_bias, col_w, col_a, col_b, row_w, row_a, row_b, mlp_in, mlp_in_a, mlp_in_b, mlp_out, mlp_out_a, mlp_out_b):
    weights = (col_w.astype(jnp.float32), row_w.astype(jnp.float32), mlp_in.astype(jnp.float32), mlp_out.astype(jnp.float32))
    adapters = tuple((stacked.astype(jnp.float32) for stacked in (col_a, col_b, row_a, row_b, mlp_in_a, mlp_in_b, mlp_out_a, mlp_out_b)))
    clip_frames = frames_in.astype(jnp.float32).reshape(CLIPS, FRAMES, D)
    clip_texts = text_states.astype(jnp.float32).reshape(CLIPS, TEXT, D)
    clip_grads = out_grad.astype(jnp.float32).reshape(CLIPS, FRAMES, D)

    def one_clip(running, pieces):
        clip_rows, clip_text, adapter_index, cotangent = pieces

        def layer(rows_in, text_in, adapter_set):
            return clip_layer(rows_in, text_in, adapter_index, norm_gain, norm_bias, weights, adapter_set)
        result, pullback = jax.vjp(layer, clip_rows, clip_text, adapters)
        grad_rows, grad_text, grad_adapters = pullback(cotangent)
        running = tuple((sofar + addend for sofar, addend in zip(running, grad_adapters)))
        return (running, (result, grad_rows, grad_text))
    empty_sums = tuple((jnp.zeros_like(stacked) for stacked in adapters))
    sums, (results, grad_frames, grad_texts) = lax.scan(one_clip, empty_sums, (clip_frames, clip_texts, adapter_pick, clip_grads))
    return (results.reshape(CLIPS * FRAMES, D).astype(jnp.bfloat16), grad_frames.reshape(CLIPS * FRAMES, D), grad_texts.reshape(CLIPS * TEXT, D), sums[0], sums[1], sums[2], sums[3], sums[4], sums[5], sums[6], sums[7])
```

```python
from functools import partial

import jax
import jax.numpy as jnp
from jax import lax
from jax.experimental import pallas as pl
from jax.experimental.pallas import tpu as pltpu
from jax.sharding import PartitionSpec as P

HEAD = 64
EPSILON = 1e-05
NEG = -1e30
BF = jnp.bfloat16
F32 = jnp.float32
C2 = 0.125 * 1.4426950408889634
SUB = 128
TILE = 256
VM = pltpu.VMEM
MESH = pl.DeviceIdType.MESH


def nn(a, b):
    return jnp.dot(a, b, preferred_element_type=F32)


def nt(a, b):
    return lax.dot_general(a, b, (((1,), (1,)), ((), ())), preferred_element_type=F32)


def tn(a, b):
    return lax.dot_general(a, b, (((0,), (0,)), ((), ())), preferred_element_type=F32)


def ring():
    t = lax.axis_index("tensor")
    core = lax.rem(t, 2)
    chip = t // 2
    p = t + 1 - 2 * core
    o = lax.rem(t + 2, 4)
    q = lax.rem(p + 2, 4)
    return t, chip, p, o, q


def meet(*others):
    barrier = pltpu.get_barrier_semaphore()
    for other in others:
        pl.semaphore_signal(barrier, inc=1, device_id={"tensor": other}, device_id_type=MESH)
    pl.semaphore_wait(barrier, len(others))


def send(src, dst, ssem, rsem, to):
    return pltpu.make_async_remote_copy(
        src, dst, ssem, rsem, device_id={"tensor": to}, device_id_type=MESH
    )


def rows(block, sub, lp):
    return pl.ds(pl.multiple_of(block * lp + sub * SUB, SUB), SUB)


def half_masks(n):
    lane = lax.broadcasted_iota(jnp.int32, (n, 128), 1)
    return lane < HEAD


class Gather:
    def __init__(self, own, held, ssem, rsem, lp):
        self.own, self.held, self.ssem, self.rsem, self.lp = own, held, ssem, rsem, lp
        self.t, self.chip, self.p, self.o, self.q = ring()
        self.subs = lp // SUB

    def near(self):
        block = pl.ds(pl.multiple_of(self.t * self.lp, SUB), self.lp)
        return send(self.own, self.held.at[block], self.ssem.at[0], self.rsem.at[0], self.p)

    def far(self, s):
        return send(
            self.own.at[pl.ds(s * SUB, SUB)],
            self.held.at[rows(self.t, s, self.lp)],
            self.ssem.at[1 + s],
            self.rsem.at[1 + s],
            self.o,
        )

    def onward(self, s):
        piece = self.held.at[rows(self.o, s, self.lp)]
        k = 1 + self.subs + s
        return send(piece, piece, self.ssem.at[k], self.rsem.at[k], self.p)

    def start(self):
        for s in range(self.subs):
            self.far(s).start()
        self.near().start()

    def finish(self):
        self.near().wait_send()
        for s in range(self.subs):
            self.far(s).wait_send()
            self.onward(s).wait_send()


class Scatter:
    def __init__(self, result, out_p, in_p, out_x, in_x, sems, lp):
        self.result, self.out_p, self.in_p, self.out_x, self.in_x = result, out_p, in_p, out_x, in_x
        self.sp, self.rp, self.sx, self.rx = sems
        self.lp = lp
        self.t, self.chip, self.p, self.o, self.q = ring()
        self.subs = lp // SUB

    def pair(self, k):
        return send(self.out_p.at[k], self.in_p.at[k], self.sp.at[k], self.rp.at[k], self.p)

    def across(self, s):
        return send(self.out_x.at[s], self.in_x.at[s], self.sx.at[s], self.rx.at[s], self.o)

    def give(self, block, s, part):
        @pl.when(block == self.q)
        def _():
            self.out_p[s] = part[...].astype(self.out_p.dtype)
            self.pair(s).start()

        @pl.when(block == self.o)
        def _():
            self.pair(s).wait_recv()
            self.out_x[s] = (part[...] + self.in_p[s].astype(F32)).astype(BF)
            self.across(s).start()

        @pl.when(block == self.p)
        def _():
            self.out_p[self.subs + s] = part[...].astype(self.out_p.dtype)
            self.pair(self.subs + s).start()

        @pl.when(block == self.t)
        def _():
            self.result[pl.ds(pl.multiple_of(s * SUB, SUB), SUB), :] = part[...]

    def finish(self):
        for s in range(self.subs):
            self.pair(self.subs + s).wait_recv()
            self.across(s).wait_recv()
            r = pl.ds(s * SUB, SUB)
            self.result[r, :] += self.in_p[self.subs + s].astype(F32) + self.in_x[s].astype(F32)
        for s in range(self.subs):
            self.pair(s).wait_send()
            self.pair(self.subs + s).wait_send()
            self.across(s).wait_send()


def scatter_scratch(lp, width, near=BF):
    n = lp // SUB
    dma = pltpu.SemaphoreType.DMA
    return [
        VM((2 * n, SUB, width), near),
        VM((2 * n, SUB, width), near),
        VM((n, SUB, width), BF),
        VM((n, SUB, width), BF),
        dma((2 * n,)),
        dma((2 * n,)),
        dma((n,)),
        dma((n,)),
    ]


def make_scatter(result, scr, lp):
    return Scatter(result, scr[0], scr[1], scr[2], scr[3], scr[4:8], lp)


def tile_rows(i):
    return pl.ds(pl.multiple_of(i * TILE, TILE), TILE)


def fill_key_aux(kaux, lp, valid):
    n = kaux.shape[0]
    row = lax.broadcasted_iota(jnp.int32, (n, 128), 0)
    lane = lax.broadcasted_iota(jnp.int32, (n, 128), 1)
    pad = lax.rem(row, lp) >= valid
    kaux[...] = jnp.where(pad & (lane == 0), NEG, 0.0).astype(BF)


def first_lane():
    lane = lax.broadcasted_iota(jnp.int32, (TILE, 128), 1)
    return jnp.where(lane == 0, 1.0, 0.0).astype(BF)


def keep(mask, value):
    return jnp.where(mask, value, jnp.zeros_like(value))


def attend_tile(i, q_ref, k_ref, v_ref, att_ref, lse_ref, kaux, qa, ss, mx, acc):
    pairs = q_ref.shape[1] // 128
    left = half_masks(TILE)
    one = first_lane()
    ri = tile_rows(i)
    for p in range(pairs):
        qp = q_ref[ri, p * 128 : p * 128 + 128]
        for a in range(2):
            m = left if a == 0 else ~left
            qa[2 * p + a] = jnp.concatenate([keep(m, qp), one], axis=1)
            mx[2 * p + a] = jnp.full((TILE, 128), NEG, F32)

    def scores(j, diagonal):
        rj = tile_rows(j)
        for p in range(pairs):
            ka = jnp.concatenate([k_ref[rj, p * 128 : p * 128 + 128], kaux[rj, :]], axis=1)
            for a in range(2):
                s = nt(qa[2 * p + a], ka)
                if diagonal:
                    row = lax.broadcasted_iota(jnp.int32, (TILE, TILE), 0)
                    lane = lax.broadcasted_iota(jnp.int32, (TILE, TILE), 1)
                    s = jnp.where(lane > row, NEG, s)
                ss[2 * p + a, :, tile_rows(j)] = s
                mx[2 * p + a] = jnp.maximum(mx[2 * p + a], jnp.maximum(s[:, :128], s[:, 128:]))

    def body(j, carry):
        scores(j, False)
        return carry

    lax.fori_loop(0, i, body, 0)
    scores(i, True)
    for h in range(2 * pairs):
        mx[h] = jnp.broadcast_to(jnp.max(mx[h], axis=1, keepdims=True) * C2, (TILE, 128))
    for p in range(pairs):
        acc[p] = jnp.zeros((TILE, 256), F32)
    ones_l = jnp.where(left, 1.0, 0.0).astype(BF)
    ones_r = jnp.where(left, 0.0, 1.0).astype(BF)

    def mix(j, carry):
        rj = tile_rows(j)
        for p in range(pairs):
            pr = []
            for a in range(2):
                m = mx[2 * p + a]
                m2 = jnp.concatenate([m, m], axis=1)
                pr.append(jnp.exp2(ss[2 * p + a, :, tile_rows(j)] * C2 - m2).astype(BF))
            vp = v_ref[rj, p * 128 : p * 128 + 128]
            va = jnp.concatenate(
                [
                    jnp.concatenate([keep(left, vp), ones_l], axis=1),
                    jnp.concatenate([keep(~left, vp), ones_r], axis=1),
                ],
                axis=0,
            )
            acc[p] += nn(jnp.concatenate(pr, axis=1), va)
        return carry

    lax.fori_loop(0, i + 1, mix, 0)
    for p in range(pairs):
        total = acc[p, :, 128:]
        att_ref[ri, p * 128 : p * 128 + 128] = (acc[p, :, :128] / total).astype(BF)
        logs = jnp.where(left, mx[2 * p], mx[2 * p + 1]) + jnp.log2(total)
        flat = logs.T
        lse_ref[pl.ds(2 * p, 1), tile_rows(i)] = flat[0:1]
        lse_ref[pl.ds(2 * p + 1, 1), tile_rows(i)] = flat[64:65]


def stack_maps(maps):
    short = 64 - sum(m.shape[0] for m in maps)
    half = list(maps)
    if short:
        half = half + [jnp.zeros((short, maps[0].shape[1]), maps[0].dtype)]
    return jnp.concatenate(half + half, axis=0)


def block_maps(maps):
    n = len(maps)
    rows_ = []
    for j, m in enumerate(maps):
        parts = [jnp.zeros_like(m)] * n
        parts[j] = m
        rows_.append(jnp.concatenate(parts, axis=1))
    return stack_maps(rows_)


def split_rank(r):
    hi = r.astype(BF)
    lo = (r - hi.astype(F32)).astype(BF)
    return jnp.where(half_masks(r.shape[0]), hi, lo)


def layer_norm(x, gain, bias):
    mean = jnp.mean(x, axis=-1, keepdims=True)
    c = x - mean
    var = jnp.mean(c * c, axis=-1, keepdims=True)
    return c * lax.rsqrt(var + EPSILON) * gain + bias


def layer_norm_back(x, gain, dy):
    mean = jnp.mean(x, axis=-1, keepdims=True)
    c = x - mean
    var = jnp.mean(c * c, axis=-1, keepdims=True)
    inv = lax.rsqrt(var + EPSILON)
    xh = c * inv
    dg = dy * gain
    m1 = jnp.mean(dg, axis=-1, keepdims=True)
    m2 = jnp.mean(dg * xh, axis=-1, keepdims=True)
    return inv * (dg - m1 - xh * m2)


def self_forward_kernel(
    lp, pick_ref, x_ref, gain_ref, bias_ref, text_ref, colw, cola, cb_ref, roww, ra_ref, rb_ref,
    res_ref, q_ref, k_ref, v_ref, att_ref, lse_ref, rank_ref, xg, small, ca_ref,
    n1, wv, wkv, cav, w0, bx, b0, a0, qa, ss, mx, acc, kaux, pf, lsem, gs, gr, ms, mr, *scr
):
    g = Gather(n1, xg, gs, gr, lp)
    sc = make_scatter(res_ref, scr, lp)
    k = pick_ref[0]
    lw = q_ref.shape[1]
    d = n1.shape[1]
    tr = text_ref.shape[0]
    rk = cb_ref.shape[2]
    loads = [pltpu.make_async_copy(cola, cav, lsem.at[0])]
    for j in range(3):
        loads.append(pltpu.make_async_copy(colw.at[j], wv.at[:, pl.ds(j * lw, lw)], lsem.at[1 + j]))
    for j in range(2):
        loads.append(pltpu.make_async_copy(colw.at[4 + j], wkv.at[:, pl.ds(j * lw, lw)], lsem.at[4 + j]))
    loads.append(pltpu.make_async_copy(roww.at[0], w0, lsem.at[6]))
    for c in loads:
        c.start()
    meet(g.p, g.o, g.q)
    valid = x_ref.shape[0]
    for s in range(g.subs):
        lo, hi = s * SUB, min(valid, s * SUB + SUB)
        y = layer_norm(x_ref[lo:hi, :].astype(F32), gain_ref[0:1, :], bias_ref[0:1, :]).astype(BF)
        if hi < lo + SUB:
            n1[lo : lo + SUB, :] = jnp.zeros((SUB, d), BF)
        n1[lo:hi, :] = y
        g.far(s).start()
    g.near().start()
    fill_key_aux(kaux, lp, valid)
    lse_ref[...] = jnp.zeros_like(lse_ref)
    loads[0].wait()
    for j in range(cav.shape[0]):
        ca_ref[j] = cav[j, k]
    wv[:, 3 * lw :] = stack_maps([ca_ref[j] for j in range(3)]).T
    bx[...] = block_maps([cb_ref[j, k] for j in range(3)])
    b0[...] = stack_maps([rb_ref[0, k]])
    a0[...] = stack_maps([ra_ref[0, k]])
    for c in loads[1:]:
        c.wait()

    def project(r, x):
        y = nn(x, wv[...])
        e = split_rank(y[:, 3 * lw :])
        rank_ref[r, :] = e
        z = nn(e, bx[...])
        q_ref[r, :] = (y[:, :lw] + z[:, :lw]).astype(BF)
        k_ref[r, :] = (y[:, lw : 2 * lw] + z[:, lw : 2 * lw]).astype(BF)
        v_ref[r, :] = (y[:, 2 * lw : 3 * lw] + z[:, 2 * lw :]).astype(BF)

    tx = text_ref[...]
    e = split_rank(nt(tx, stack_maps([ca_ref[4], ca_ref[5]])))
    kv = nn(tx, wkv[...]) + nn(e, block_maps([cb_ref[4, k], cb_ref[5, k]]))
    small[g.t, :tr, :] = kv[:, :lw].astype(BF)
    small[g.t, tr : 2 * tr, :] = kv[:, lw:].astype(BF)
    small[g.t, 2 * tr : 2 * tr + rk, :] = cb_ref[3, k]
    small[g.t, 2 * tr + rk :, :] = ra_ref[1, k]

    def message(i, to):
        return send(small.at[g.t], small.at[g.t], ms.at[i], mr.at[i], to)

    message(0, g.p).start()
    message(1, g.o).start()
    message(2, g.q).start()

    r = pl.ds(pl.multiple_of(g.t * lp, SUB), lp)
    xg[r, :] = n1[...]
    project(r, n1[...])
    g.near().wait_recv()
    r = pl.ds(pl.multiple_of(g.p * lp, SUB), lp)
    project(r, xg[r, :])

    def arrive(s, carry):
        g.far(s).wait_recv()
        g.onward(s).start()
        r = rows(g.o, s, lp)
        project(r, xg[r, :])
        g.onward(s).wait_recv()
        r = rows(g.q, s, lp)
        project(r, xg[r, :])
        return carry

    lax.fori_loop(0, g.subs, arrive, 0)
    half = q_ref.shape[0] // (2 * TILE)

    def step(n, carry):
        second = n // half
        i = half * ((1 - g.chip) + second * (2 * g.chip - 1)) + lax.rem(n, half)
        attend_tile(i, q_ref, k_ref, v_ref, att_ref, lse_ref, kaux, qa, ss, mx, acc)
        a = att_ref[tile_rows(i), :]
        e = split_rank(nt(a, a0[...]))
        pf[...] = nn(a, w0[...]) + nn(e, b0[...])
        for c in range(TILE // SUB):
            chunk = i * (TILE // SUB) + c
            sc.give(chunk // g.subs, lax.rem(chunk, g.subs), pf.at[pl.ds(c * SUB, SUB)])
        return carry

    lax.fori_loop(0, 2 * half, step, 0)
    sc.finish()
    g.finish()
    for i, to in enumerate((g.p, g.o, g.q)):
        message(i, to).wait()


def vspec():
    return pl.BlockSpec(memory_space=VM)


def params(cid, vmem=60):
    return pltpu.CompilerParams(
        collective_id=cid, has_side_effects=True, vmem_limit_bytes=vmem * 2**20
    )


def cost(flops, nbytes):
    return pl.CostEstimate(flops=int(flops), bytes_accessed=int(nbytes), transcendentals=0)


def sspec():
    return pl.BlockSpec(memory_space=pltpu.SMEM)


def aspec():
    return pl.BlockSpec(memory_space=pl.ANY)


def self_forward(pick, x, gain, bias, text, colw, cola, cb, roww, ra, rb):
    valid, d = x.shape
    lp = -(-valid // SUB) * SUB
    lw = colw.shape[2]
    n = 4 * lp
    heads = lw // HEAD
    rk = cb.shape[2]
    sds = jax.ShapeDtypeStruct
    nsem = 1 + 2 * (lp // SUB)
    dma = pltpu.SemaphoreType.DMA
    return pl.pallas_call(
        partial(self_forward_kernel, lp),
        out_shape=[
            sds((lp, d), F32),
            sds((n, lw), BF),
            sds((n, lw), BF),
            sds((n, lw), BF),
            sds((n, lw), BF),
            sds((8, n), F32),
            sds((n, 128), BF),
            sds((n, d), BF),
            sds((4, 2 * text.shape[0] + 2 * rk, lw), BF),
            sds((cola.shape[0],) + cola.shape[2:], BF),
        ],
        in_specs=[sspec()] + [vspec()] * 4 + [aspec()] * 2 + [vspec()] + [aspec()] + [vspec()] * 2,
        out_specs=[vspec()] * 10,
        scratch_shapes=[
            VM((lp, d), BF),
            VM((d, 3 * lw + 128), BF),
            VM((d, 2 * lw), BF),
            VM(cola.shape, BF),
            VM((lw, d), BF),
            VM((128, 3 * lw), BF),
            VM((128, d), BF),
            VM((128, lw), BF),
            VM((heads, TILE, 256), BF),
            VM((heads, TILE, n), F32),
            VM((heads, TILE, 128), F32),
            VM((heads // 2, TILE, 256), F32),
            VM((n, 128), BF),
            VM((TILE, d), F32),
            dma((7,)),
            dma((nsem,)),
            dma((nsem,)),
            dma((3,)),
            dma((3,)),
        ]
        + scatter_scratch(lp, d, F32),
        compiler_params=params(1, 63),
        cost_estimate=cost(2 * n * d * 1280, n * d * 8),
        name="self_forward",
    )(pick, x, gain, bias, text, colw, cola, cb, roww, ra, rb)


def states(small, p, lo, n):
    per = small.shape[2] // 128
    x = small[p // per, lo : lo + n, pl.ds(pl.multiple_of(lax.rem(p, per) * 128, 128), 128)]
    left = half_masks(n)
    return jnp.concatenate([keep(left, x), keep(~left, x)], axis=0)


def whole_map(small, lo, n):
    return jnp.concatenate([small[i, lo : lo + n, :] for i in range(small.shape[0])], axis=1)


def pair_ones(n):
    left = half_masks(2 * n)
    row = lax.broadcasted_iota(jnp.int32, (2 * n, 128), 0)
    return jnp.where((row < n) == left, 1.0, 0.0).astype(BF)


def cross_scores(cqp, kst):
    s = nt(cqp, kst)
    left = half_masks(s.shape[0])
    m0 = jnp.max(jnp.where(left, s, NEG), axis=1, keepdims=True)
    m1 = jnp.max(jnp.where(left, NEG, s), axis=1, keepdims=True)
    return jnp.exp2((s - jnp.where(left, m0, m1)) * C2)


def cross_forward_kernel(
    tr, rk, pick_ref, out0_ref, x_ref, gain_ref, bias_ref, colw, roww, got, small, ca_ref, rb_ref,
    first_ref, n2_ref, cq_ref, cm_ref, second_ref, n3_ref, wcf, wrf, wc, wr, lsem, ssem, rsem, osem,
):
    t, chip, p, o, q = ring()
    k = pick_ref[0]
    lp, d = first_ref.shape
    valid = x_ref.shape[0]
    lw = wc.shape[2]
    share = got.shape[0]
    piece = got.shape[1] // 2

    def block(i):
        return pl.ds(pl.multiple_of(i * lw, 128), lw)

    mine = [pltpu.make_async_copy(colw.at[3], wc.at[t], lsem.at[0])]
    for i in range(share):
        mine.append(
            pltpu.make_async_copy(got.at[i, pl.ds(0, piece)], wc.at[o, pl.ds(i * piece, piece)], lsem.at[1 + i])
        )
    other = [pltpu.make_async_copy(roww.at[1], wr.at[block(t)], lsem.at[1 + share])]
    for i in range(share):
        col, row = i * piece // lw, i * piece % lw
        dst = wr.at[pl.ds(pl.multiple_of(o * lw + row, 64), piece), pl.ds(col * lw, lw)]
        other.append(pltpu.make_async_copy(got.at[i, pl.ds(piece, piece)], dst, lsem.at[2 + share + i]))
    for c in mine + other:
        c.start()
    meet(p)

    def swap(i):
        ref = (wc.at[t], wc.at[o], wr.at[block(t)], wr.at[block(o)])[i]
        return send(ref, ref, ssem.at[i], rsem.at[i], p)

    for s in range(lp // SUB):
        lo, hi = s * SUB, min(valid, s * SUB + SUB)
        if hi < lo + SUB:
            first_ref[lo : lo + SUB, :] = out0_ref[lo : lo + SUB, :]
        first_ref[lo:hi, :] = x_ref[lo:hi, :].astype(F32) + out0_ref[lo:hi, :]
        n2_ref[lo : lo + SUB, :] = layer_norm(
            first_ref[lo : lo + SUB, :], gain_ref[1:2, :], bias_ref[1:2, :]
        ).astype(BF)
        if s == 0:
            for c in mine:
                c.wait()
            swap(0).start()
            swap(1).start()
        if s == 1:
            for c in other:
                c.wait()
            swap(2).start()
            swap(3).start()
    n2 = n2_ref[...]
    e3 = split_rank(nt(n2, stack_maps([ca_ref[3]])))

    def project(i):
        b3 = stack_maps([small[i, 2 * tr : 2 * tr + rk, :]])
        cq_ref[:, block(i)] = (nn(n2, wc[i]) + nn(e3, b3)).astype(BF)

    project(t)
    project(o)
    swap(0).wait_recv()
    project(p)
    swap(1).wait_recv()
    project(q)
    ones = pair_ones(tr)

    def attend(j, carry):
        cols = pl.ds(pl.multiple_of(j * 128, 128), 128)
        pr = cross_scores(cq_ref[:, cols], states(small, j, 0, tr)).astype(BF)
        ov = nn(pr, jnp.concatenate([states(small, j, tr, tr), ones], axis=1))
        cm_ref[:, cols] = (ov[:, :128] / ov[:, 128:]).astype(BF)
        return carry

    lax.fori_loop(0, d // 128, attend, 0)
    swap(2).wait_recv()
    swap(3).wait_recv()
    keepc = [pltpu.make_async_copy(wc, wcf, osem.at[0]), pltpu.make_async_copy(wr, wrf, osem.at[1])]
    for c in keepc:
        c.start()
    cm = cm_ref[...]
    e1 = split_rank(nt(cm, stack_maps([whole_map(small, 2 * tr + rk, rk)])))
    second_ref[...] = first_ref[...] + nn(cm, wr[...]) + nn(e1, stack_maps([rb_ref[1, k]]))
    for s in range(lp // SUB):
        r = pl.ds(s * SUB, SUB)
        n3_ref[r, :] = layer_norm(second_ref[r, :], gain_ref[2:3, :], bias_ref[2:3, :]).astype(BF)
    for i in range(4):
        swap(i).wait_send()
    for c in keepc:
        c.wait()


def cross_forward(tr, rk, pick, out0, x, gain, bias, colw, roww, got, small, ca, rb):
    lp, d = out0.shape
    lw = colw.shape[2]
    share = got.shape[0]
    sds = jax.ShapeDtypeStruct
    dma = pltpu.SemaphoreType.DMA
    return pl.pallas_call(
        partial(cross_forward_kernel, tr, rk),
        out_shape=[
            sds((lp, d), F32),
            sds((lp, d), BF),
            sds((lp, d), BF),
            sds((lp, d), BF),
            sds((lp, d), F32),
            sds((lp, d), BF),
            sds((4, d, lw), BF),
            sds((4 * lw, d), BF),
        ],
        in_specs=[sspec()] + [vspec()] * 4 + [aspec()] * 3 + [vspec()] * 3,
        out_specs=[vspec()] * 6 + [aspec()] * 2,
        scratch_shapes=[
            VM((4, d, lw), BF),
            VM((4 * lw, d), BF),
            dma((2 + 2 * share,)),
            dma((4,)),
            dma((4,)),
            dma((2,)),
        ],
        compiler_params=params(4),
        cost_estimate=cost(4 * lp * d * d, 6 * d * d),
        name="cross_forward",
    )(pick, out0, x, gain, bias, colw, roww, got, small, ca, rb)


def cross_backward_kernel(
    tr, rk, pick_ref, gn3_ref, out3_ref, og_ref, second_ref, first_ref, n2_ref, cq_ref, cm_ref, gain_ref, wc_hbm, wr_hbm,
    small, ca_ref, rb_ref,
    gf_ref, gb_ref, dk_ref, dv_ref, a3g_ref, b3g_ref, a1g_ref, b1g_ref, block_ref,
    wc, wr, gs, g, gcm, dcq, gn2, lsem,
):
    loads = [
        pltpu.make_async_copy(wr_hbm, wr, lsem.at[0]),
        pltpu.make_async_copy(wc_hbm, wc, lsem.at[1]),
    ]
    for c in loads:
        c.start()
    k = pick_ref[0]
    lp, d = og_ref.shape
    for s in range(lp // SUB):
        r = pl.ds(s * SUB, SUB)
        v = og_ref[r, :].astype(F32) + layer_norm_back(second_ref[r, :], gain_ref[2:3, :], gn3_ref[r, :])
        gs[r, :] = v
        g[r, :] = v.astype(BF)
        ok = slice(s * SUB, min(block_ref.shape[0], s * SUB + SUB))
        block_ref[ok, :] = (second_ref[ok, :] + out3_ref[ok, :]).astype(BF)
    loads[0].wait()
    a1 = stack_maps([whole_map(small, 2 * tr + rk, rk)])
    b1 = stack_maps([rb_ref[1, k]])
    e1 = split_rank(nt(g[...], b1))
    gcm[...] = (nt(g[...], wr[...]) + nn(e1, a1)).astype(BF)
    ones = pair_ones(tr)

    def attend(j, carry):
        cols = pl.ds(pl.multiple_of(j * 128, 128), 128)
        kst = states(small, j, 0, tr)
        cqp, gp = cq_ref[:, cols], gcm[:, cols]
        pr = cross_scores(cqp, kst)
        pr = pr / nn(pr.astype(BF), ones)
        low = pr.astype(BF)
        dp = nt(gp, states(small, j, tr, tr))
        pd = pr * dp
        hi = pd.astype(BF)
        lo = (pd - hi.astype(F32)).astype(BF)
        mean = nn(jnp.concatenate([hi, lo], axis=1), jnp.concatenate([ones, ones], axis=0))
        ds = (pr * (dp - mean)).astype(BF)
        dcq[:, cols] = (nn(ds, kst) * 0.125).astype(BF)
        dk = tn(ds, cqp)
        dv = tn(low, gp)
        left = half_masks(tr)
        dk_ref[:, cols] = jnp.where(left, dk[:tr], dk[tr:]) * 0.125
        dv_ref[:, cols] = jnp.where(left, dv[:tr], dv[tr:])
        return carry

    lax.fori_loop(0, d // 128, attend, 0)
    loads[1].wait()
    lw = wc.shape[2]
    a3 = stack_maps([ca_ref[3]])
    e3 = split_rank(nt(dcq[...], stack_maps([whole_map(small, 2 * tr, rk)])))
    gn2[...] = nn(e3, a3)
    for t in range(wc.shape[0]):
        gn2[...] += nt(dcq[:, t * lw : t * lw + lw], wc[t])
    for s in range(lp // SUB):
        r = pl.ds(s * SUB, SUB)
        v = gs[r, :] + layer_norm_back(first_ref[r, :], gain_ref[1:2, :], gn2[r, :])
        gf_ref[r, :] = v
        gb_ref[r, :] = v.astype(BF)
    a3g_ref[...] = tn(e3, n2_ref[...])[:rk]
    b3g_ref[...] = tn(nt(n2_ref[...], a3).astype(BF), dcq[...])[:rk]
    a1g_ref[...] = tn(e1, cm_ref[...])[:rk]
    b1g_ref[...] = tn(nt(cm_ref[...], a1).astype(BF), g[...])[:rk]


def cross_backward(valid, tr, rk, pick, gn3, out3, og, second, first, n2, cq, cm, gain, wc, wr, small, ca, rb):
    lp, d = og.shape
    sds = jax.ShapeDtypeStruct
    return pl.pallas_call(
        partial(cross_backward_kernel, tr, rk),
        out_shape=[
            sds((lp, d), F32),
            sds((lp, d), BF),
            sds((tr, d), F32),
            sds((tr, d), F32),
        ]
        + [sds((rk, d), F32)] * 4 + [sds((valid, d), BF)],
        in_specs=[sspec()] + [vspec()] * 9 + [aspec()] * 2 + [vspec()] * 3,
        out_specs=[vspec()] * 9,
        scratch_shapes=[
            VM(wc.shape, BF),
            VM(wr.shape, BF),
            VM((lp, d), F32),
            VM((lp, d), BF),
            VM((lp, d), BF),
            VM((lp, d), BF),
            VM((lp, d), F32),
            pltpu.SemaphoreType.DMA((3,)),
        ],
        compiler_params=pltpu.CompilerParams(vmem_limit_bytes=60 * 2**20),
        cost_estimate=cost(4 * lp * d * d, 6 * d * d),
        name="cross_backward",
    )(pick, gn3, out3, og, second, first, n2, cq, cm, gain, wc, wr, small, ca, rb)


def mlp_kernel(
    lp, pick_ref, n3_ref, og_hbm, win_hbm, wout_hbm, ia_hbm, ib_hbm, oa_hbm, ob_hbm,
    gn_ref, out_ref, iag_ref, ibg_ref, oag_ref, obg_ref, own_ref,
    xg, og, win, wout, wt, hid, gp, bro, pf, maps, lsem, gs, gr, *scr
):
    g = Gather(n3_ref, xg, gs, gr, lp)
    half = len(scr) // 2
    sc1 = make_scatter(gn_ref, scr[:half], lp)
    sc2 = make_scatter(out_ref, scr[half:], lp)
    loads = [
        pltpu.make_async_copy(wout_hbm, wout, lsem.at[0]),
        pltpu.make_async_copy(og_hbm, og, lsem.at[1]),
        pltpu.make_async_copy(win_hbm, win, lsem.at[2]),
    ]
    for i, m in enumerate((ia_hbm, ib_hbm, oa_hbm, ob_hbm)):
        loads.append(pltpu.make_async_copy(m, maps.at[i], lsem.at[3 + i]))
    k = pick_ref[0]
    for c in loads:
        c.start()
    meet(g.p, g.o)
    g.start()
    n, d = xg.shape
    nb = n // lp
    for c in loads:
        c.wait()
    rk = maps.shape[2]
    ia, ib, oa, ob = maps[0, k], maps[1, k], maps[2, k], maps[3, k]
    valid = og.shape[0] // nb
    cut = valid // SUB * SUB
    for b in range(nb):

        @pl.when(g.t == b)
        def _():
            own_ref[cut:, :] = jnp.zeros((lp - cut, d), BF)
            own_ref[:valid, :] = og[b * valid : b * valid + valid, :]

    for c in range(wout.shape[0] // 128):
        r = slice(c * 128, c * 128 + 128)
        wout[r, :] = (wout[r, :].astype(F32) + tn(oa[:, r], ob)).astype(BF)
    obw = stack_maps([ob])
    ibw = stack_maps([ib])

    for b in range(nb):
        r = slice(b * lp, b * lp + valid)
        x = og[b * valid : b * valid + valid, :]
        gp[b * lp + cut : b * lp + lp, :] = jnp.zeros((lp - cut, gp.shape[1]), BF)
        gp[r, :] = nt(x, wout[...]).astype(BF)
        bro[b * lp + cut : b * lp + lp, :] = jnp.zeros((lp - cut, 128), BF)
        bro[r, :] = nt(x, obw).astype(BF)
    for c in range(win.shape[1] // 128):
        cs = slice(c * 128, c * 128 + 128)
        w = (win[:, cs].astype(F32) + tn(ia, ib[:, cs])).astype(BF)
        win[:, cs] = w
        wt[cs, :] = w.T
    wid = 256

    def inner(r, m):
        def col(c, carry):
            cs = pl.ds(pl.multiple_of(c * wid, wid), wid)
            pre = nn(xg[r, :], win[:, cs])
            cdf = 0.5 * lax.erf(pre * 0.7071067811865476) + 0.5
            slope = cdf + pre * (0.3989422804014327 * jnp.exp(-0.5 * pre * pre))
            hid[r, cs] = (pre * cdf).astype(BF)
            gp[r, cs] = (gp[r, cs].astype(F32) * slope).astype(BF)
            return carry

        lax.fori_loop(0, win.shape[1] // wid, col, 0)

    r = pl.ds(pl.multiple_of(g.t * lp, SUB), lp)
    xg[r, :] = n3_ref[...]
    inner(r, lp)
    g.near().wait_recv()
    r = pl.ds(pl.multiple_of(g.p * lp, SUB), lp)
    inner(r, lp)

    def arrive(s, carry):
        g.far(s).wait_recv()
        g.onward(s).start()
        inner(rows(g.o, s, lp), SUB)
        g.onward(s).wait_recv()
        inner(rows(g.q, s, lp), SUB)
        for b in (g.q, g.o):
            pf[...] = nn(gp[rows(b, s, lp), :], wt[...])
            sc1.give(b, s, pf)
        return carry

    lax.fori_loop(0, g.subs, arrive, 0)

    def near1(s, carry):
        for b in (g.p, g.t):
            pf[...] = nn(gp[rows(b, s, lp), :], wt[...])
            sc1.give(b, s, pf)
        return carry

    lax.fori_loop(0, g.subs, near1, 0)

    def far2(s, carry):
        for b in (g.q, g.o):
            pf[...] = nn(hid[rows(b, s, lp), :], wout[...])
            sc2.give(b, s, pf)
        return carry

    lax.fori_loop(0, g.subs, far2, 0)

    def near2(s, carry):
        for b in (g.p, g.t):
            pf[...] = nn(hid[rows(b, s, lp), :], wout[...])
            sc2.give(b, s, pf)
        return carry

    lax.fori_loop(0, g.subs, near2, 0)
    rank = nt(xg[...], stack_maps([ia])).astype(BF)
    ibg_ref[...] = tn(rank, gp[...])[:rk]
    iag_ref[...] = tn(nt(gp[...], ibw).astype(BF), xg[...])[:rk]
    oag_ref[...] = tn(bro[...], hid[...])[:rk]
    obg_ref[...] = jnp.zeros_like(obg_ref)
    oaw = stack_maps([oa])
    for b in range(nb):
        rank = nt(hid[b * lp : b * lp + valid, :], oaw).astype(BF)
        obg_ref[...] += tn(rank, og[b * valid : b * valid + valid, :])[:rk]
    sc1.finish()
    sc2.finish()
    g.finish()


def mlp(pick, n3, og, win, wout, ia, ib, oa, ob):
    lp, d = n3.shape
    f = win.shape[1]
    rk = ia.shape[1]
    n = 4 * lp
    sds = jax.ShapeDtypeStruct
    nsem = 1 + 2 * (lp // SUB)
    dma = pltpu.SemaphoreType.DMA
    return pl.pallas_call(
        partial(mlp_kernel, lp),
        out_shape=[
            sds((lp, d), F32),
            sds((lp, d), F32),
            sds((rk, d), F32),
            sds((rk, f), F32),
            sds((rk, f), F32),
            sds((rk, d), F32),
            sds((lp, d), BF),
        ],
        in_specs=[sspec(), vspec()] + [aspec()] * 7,
        out_specs=[vspec()] * 7,
        scratch_shapes=[
            VM((n, d), BF),
            VM(og.shape, BF),
            VM((d, f), BF),
            VM((f, d), BF),
            VM((f, d), BF),
            VM((n, f), BF),
            VM((n, f), BF),
            VM((n, 128), BF),
            VM((SUB, d), F32),
            VM((4,) + ia.shape, BF),
            dma((7,)),
            dma((nsem,)),
            dma((nsem,)),
        ]
        + scatter_scratch(lp, d)
        + scatter_scratch(lp, d),
        compiler_params=params(3, 63),
        cost_estimate=cost(8 * n * d * f, n * d * 16),
        name="mlp_both",
    )(pick, n3, og, win, wout, ia, ib, oa, ob)


def self_backward_kernel(
    lp, ndp, pick_ref, g_ref, roww, colw, ca_ref, cb_ref, ra_ref, rb_ref, q_ref, k_ref, v_ref, att_ref, lse_ref,
    n1_hbm, rank_ref, gain_ref, text_ref, x_ref, gf_hbm, dk_ref, dv_ref,
    a3g_ref, b3g_ref, a1g_ref, b1g_ref, iag_ref, ibg_ref, oag_ref, obg_ref,
    frames_ref, tg_ref, got_a, got_b, got_c, got_e, got_l,
    res_ref, gg, do, dqa, dka, dva, dqkv, kaux, delta,
    w0, wt, n1v, br0, br, ax, bx, a0, b0, pf,
    wkv, gkv, tsend, trecv, e1s, e1r, e2s, e2r, ls, lr, pa, pb, pc, eh, lh,
    lsem, gs, gr, ms, mr, ds_, dr, osem, xs, xr, *scr
):
    g = Gather(g_ref, gg, gs, gr, lp)
    sc = make_scatter(res_ref, scr, lp)
    k = pick_ref[0]
    lw = q_ref.shape[1]
    loads = [pltpu.make_async_copy(roww.at[0], w0, lsem.at[0])]
    for j in range(3):
        loads.append(pltpu.make_async_copy(colw.at[j], n1v.at[:, pl.ds(j * lw, lw)], lsem.at[1 + j]))
    later = pltpu.make_async_copy(n1_hbm, n1v, lsem.at[5])
    for j in range(2):
        loads.append(pltpu.make_async_copy(colw.at[4 + j], wkv.at[:, pl.ds(j * lw, lw)], lsem.at[6 + j]))
    valid = x_ref.shape[0]
    d = g_ref.shape[1]
    tr = text_ref.shape[0]
    rk = cb_ref.shape[2]
    tq = tr // 4
    me = lax.axis_index("dp")
    core = lax.rem(g.t, 2)
    peers = ((g.p, 1 - core), (g.o, core), (g.q, 1 - core))
    he, hl = eh.shape[0], lh.shape[0]

    def to_peers(kind, i):
        to, c = peers[i]
        if kind == 0:
            src, dst = e1s.at[to], e1r.at[g.t]
        elif kind == 1:
            src, dst = e2s.at[pl.ds(pl.multiple_of(c * he, 16), he)], e2r.at[g.t]
        elif kind == 2:
            src, dst = tsend.at[pl.ds(pl.multiple_of(to * tq, 16), tq)], trecv.at[g.t]
        else:
            src, dst = ls.at[pl.ds(pl.multiple_of(c * hl, 16), hl)], lr.at[g.t]
        return send(src, dst, ms.at[kind, i], mr.at[kind, i], to)

    pushes = (
        (pa, got_a.at[me]),
        (pb, got_b.at[me]),
        (pc, got_c.at[me]),
        (eh, got_e.at[core, me]),
        (lh, got_l.at[core, me]),
    )

    def push(kind, i):
        src, dst = pushes[kind]
        to = lax.rem(me + i, ndp)
        return pltpu.make_async_remote_copy(
            src, dst, ds_.at[kind, i], dr.at[kind, i], device_id={"dp": to}, device_id_type=MESH
        )

    def push_all(kind):
        src, dst = pushes[kind]
        pltpu.make_async_copy(src, dst, osem.at[kind]).start()

        def one_push(i, carry):
            push(kind, i).start()
            return carry

        lax.fori_loop(1, ndp, one_push, 0)

    def pushed(kind):
        src, dst = pushes[kind]
        pltpu.make_async_copy(src, dst, osem.at[kind]).wait()

        def one_wait(i, carry):
            push(kind, i).wait()
            return carry

        lax.fori_loop(1, ndp, one_wait, 0)

    def to_partner(kind):
        ref = (got_e, got_l)[kind].at[core]
        return send(ref, ref, xs.at[kind], xr.at[kind], g.p)
    for c in loads:
        c.start()
    barrier = pltpu.get_barrier_semaphore()
    for other, _ in peers:
        pl.semaphore_signal(barrier, inc=1, device_id={"tensor": other}, device_id_type=MESH)

    def greet(i, carry):
        pl.semaphore_signal(barrier, inc=1, device_id={"dp": lax.rem(me + i, ndp)}, device_id_type=MESH)
        return carry

    lax.fori_loop(1, ndp, greet, 0)
    pl.semaphore_wait(barrier, 3 + ndp - 1)
    g.start()
    for i in range(4):
        c = slice(i * lw, i * lw + lw)
        e1s[i, :tr, :] = dk_ref[:, c].astype(BF)
        e1s[i, tr : 2 * tr, :] = dv_ref[:, c].astype(BF)
        e1s[i, 2 * tr : 2 * tr + rk, :] = b3g_ref[:, c].astype(BF)
        e1s[i, 2 * tr + rk :, :] = a1g_ref[:, c].astype(BF)
    for i in range(3):
        to_peers(0, i).start()
    pa[:rk, :] = ibg_ref[...].astype(BF)
    pa[rk:, :] = oag_ref[...].astype(BF)
    push_all(0)
    n = q_ref.shape[0]
    pairs = lw // 128
    fill_key_aux(kaux, lp, valid)
    left = half_masks(TILE)
    one = first_lane()
    dqa[...] = jnp.zeros_like(dqa)
    delta[...] = jnp.zeros_like(delta)

    a0[...] = stack_maps([ra_ref[0, k]])
    b0[...] = stack_maps([rb_ref[0, k]])
    bx[...] = block_maps([cb_ref[j, k] for j in range(3)])
    loads[0].wait()

    def back(r, x):
        e = split_rank(nt(x, b0[...]))
        br0[r, :] = e
        do[r, :] = (nt(x, w0[...]) + nn(e, a0[...])).astype(BF)

    r = pl.ds(pl.multiple_of(g.t * lp, SUB), lp)
    gg[r, :] = g_ref[...]
    back(r, g_ref[...])
    g.near().wait_recv()
    r = pl.ds(pl.multiple_of(g.p * lp, SUB), lp)
    back(r, gg[r, :])
    for c in loads[1:]:
        c.wait()
    ax[...] = stack_maps([ca_ref[j] for j in range(3)])
    for c in range(3 * lw // 128):
        wt[c * 128 : c * 128 + 128, :] = n1v[:, c * 128 : c * 128 + 128].T
    later.start()

    def arrive(s, carry):
        g.far(s).wait_recv()
        g.onward(s).start()
        g.onward(s).wait_recv()
        return carry

    lax.fori_loop(0, g.subs, arrive, 0)
    for b in (g.o, g.q):
        r = pl.ds(pl.multiple_of(b * lp, SUB), lp)
        back(r, gg[r, :])
    lane = lax.broadcasted_iota(jnp.int32, (8, 128), 1)
    row = lax.broadcasted_iota(jnp.int32, (8, 128), 0)
    pick = jnp.where((lane // HEAD) == row, 1.0, 0.0).astype(BF)
    pick = jnp.concatenate([pick, pick], axis=1)

    def deltas(i, carry):
        r = tile_rows(i)
        for p in range(pairs):
            cols = slice(p * 128, p * 128 + 128)
            pr = do[r, cols].astype(F32) * att_ref[r, cols].astype(F32)
            hi = pr.astype(BF)
            lo = (pr - hi.astype(F32)).astype(BF)
            both = nt(pick, jnp.concatenate([hi, lo], axis=1))
            delta[pl.ds(2 * p, 2), r] = both[0:2]
        return carry

    lax.fori_loop(0, n // TILE, deltas, 0)

    own = pl.ds(pl.multiple_of(g.t * lw, 128), lw)

    def first_stage():
        for i in range(3):
            to_peers(0, i).wait_recv()
        near = [e1r[to] for to, _ in peers]

        def total(ref, lo, hi):
            y = ref[:, own]
            for b in near:
                y = y + b[lo:hi, :].astype(F32)
            return y

        gkv[:, :lw] = total(dk_ref, 0, tr).astype(BF)
        gkv[:, lw:] = total(dv_ref, tr, 2 * tr).astype(BF)
        pb[:rk, :] = total(b3g_ref, 2 * tr, 2 * tr + rk).astype(BF)
        pb[3 * rk : 4 * rk, :] = total(a1g_ref, 2 * tr + rk, 2 * tr + 2 * rk).astype(BF)
        tx = text_ref[...]
        a45 = stack_maps([ca_ref[4], ca_ref[5]])
        e = split_rank(nt(gkv[...], block_maps([cb_ref[4, k], cb_ref[5, k]])))
        tsend[...] = (nt(gkv[...], wkv[...]) + nn(e, a45)).astype(BF)
        ag45 = tn(e, tx)
        bg45 = tn(nt(tx, a45).astype(BF), gkv[...])
        pb[rk : 2 * rk, :] = bg45[:rk, :lw].astype(BF)
        pb[2 * rk : 3 * rk, :] = bg45[rk : 2 * rk, lw:].astype(BF)
        r0 = nt(att_ref[...], a0[...]).astype(BF)
        pb[4 * rk : 5 * rk, :] = tn(br0[...], att_ref[...])[:rk].astype(BF)
        slot = lax.broadcasted_iota(jnp.int32, (pb.shape[0] - 5 * rk, lw), 0)
        pb[5 * rk :, :] = jnp.where(slot == k, 1.0, 0.0).astype(BF)
        terms = (a3g_ref[...], ag45[:rk], ag45[rk : 2 * rk], tn(r0, gg[...])[:rk], b1g_ref[...], iag_ref[...], obg_ref[...])
        for i, m in enumerate(terms):
            e2s[i * rk : i * rk + rk, :] = m.astype(BF)
        e2s[len(terms) * rk :, :] = jnp.zeros((e2s.shape[0] - len(terms) * rk, d), BF)
        for i in range(3):
            to_peers(1, i).start()
            to_peers(2, i).start()

    def second_stage():
        for i in range(3):
            to_peers(1, i).wait_recv()
            to_peers(2, i).wait_recv()
        y = e2s[pl.ds(pl.multiple_of(core * he, 16), he), :].astype(F32)
        z = tsend[pl.ds(pl.multiple_of(g.t * tq, 16), tq), :].astype(F32)
        for to, _ in peers:
            y = y + e2r[to].astype(F32)
            z = z + trecv[to].astype(F32)
        eh[...] = y.astype(BF)
        tg_ref[...] = z
        push_all(1)
        push_all(3)

    def column(j, carry):
        pl.when(j == 1)(first_stage)
        pl.when(j == 2)(second_stage)
        rj = tile_rows(j)
        dka[...] = jnp.zeros_like(dka)
        dva[...] = jnp.zeros_like(dva)

        def block(i, diagonal):
            ri = tile_rows(i)
            for p in range(pairs):
                cols = slice(p * 128, p * 128 + 128)
                kp, vp, qp, dop = k_ref[rj, cols], v_ref[rj, cols], q_ref[ri, cols], do[ri, cols]
                qx = jnp.concatenate([qp, one], axis=1)
                aux = kaux[rj, :]
                pts, dss = [], []
                for a in range(2):
                    m = left if a == 0 else ~left
                    h = 2 * p + a
                    st = nt(jnp.concatenate([keep(m, kp), aux], axis=1), qx)
                    if diagonal:
                        kr = lax.broadcasted_iota(jnp.int32, (TILE, TILE), 0)
                        qc = lax.broadcasted_iota(jnp.int32, (TILE, TILE), 1)
                        st = jnp.where(kr > qc, NEG, st)
                    dp = nt(keep(m, vp), dop)
                    pt = jnp.exp2(st * C2 - lse_ref[pl.ds(h, 1), ri])
                    pts.append(pt.astype(BF))
                    dss.append((pt * (dp - delta[pl.ds(h, 1), ri])).astype(BF))
                do2 = jnp.concatenate([keep(left, dop), keep(~left, dop)], axis=0)
                q2 = jnp.concatenate([keep(left, qp), keep(~left, qp)], axis=0)
                k2 = jnp.concatenate([keep(left, kp), keep(~left, kp)], axis=0)
                dva[:, cols] += nn(jnp.concatenate(pts, axis=1), do2)
                dka[:, cols] += nn(jnp.concatenate(dss, axis=1), q2)
                dqa[ri, cols] += tn(jnp.concatenate(dss, axis=0), k2)

        block(j, True)

        def body(i, c):
            block(i, False)
            return c

        lax.fori_loop(j + 1, n // TILE, body, 0)
        dqkv[rj, lw : 2 * lw] = (dka[...] * 0.125).astype(BF)
        dqkv[rj, 2 * lw :] = dva[...].astype(BF)
        return carry

    lax.fori_loop(0, n // TILE, column, 0)

    def close(i, carry):
        r = tile_rows(i)
        dqkv[r, :lw] = (dqa[r, :] * 0.125).astype(BF)
        return carry

    lax.fori_loop(0, n // TILE, close, 0)

    br[...] = split_rank(nt(dqkv[...], bx[...]))
    later.wait()
    ls[...] = tn(br[...], n1v[...])[: ls.shape[0]].astype(BF)
    cbg = tn(rank_ref[...], dqkv[...])
    for j in range(3):
        pc[j * rk : j * rk + rk, :] = cbg[j * rk : j * rk + rk, j * lw : j * lw + lw].astype(BF)
    for i in range(3):
        to_peers(3, i).start()
    push_all(2)

    def term(b, s):
        r = rows(b, s, lp)
        pf[...] = nn(dqkv[r, :], wt[...]) + nn(br[r, :], ax[...])
        sc.give(b, s, pf)

    def step(s, carry):
        for b in (g.q, g.o):
            term(b, s)
        return carry

    lax.fori_loop(0, g.subs, step, 0)

    for i in range(3):
        to_peers(3, i).wait_recv()
    y = ls[pl.ds(pl.multiple_of(core * hl, 16), hl), :].astype(F32)
    for to, _ in peers:
        y = y + lr[to].astype(F32)
    lh[...] = y.astype(BF)
    push_all(4)

    def step2(s, carry):
        for b in (g.p, g.t):
            term(b, s)
        return carry

    lax.fori_loop(0, g.subs, step2, 0)
    pushed(3)
    to_partner(0).start()
    sc.finish()
    for s in range(lp // SUB):
        bring = pltpu.make_async_copy(gf_hbm.at[pl.ds(s * SUB, SUB)], pf, lsem.at[4])
        bring.start()
        bring.wait()
        r = slice(s * SUB, min(valid, s * SUB + SUB))
        frames_ref[r, :] = pf[: r.stop - r.start, :] + layer_norm_back(x_ref[r, :].astype(F32), gain_ref[0:1, :], res_ref[r, :])
    pushed(4)
    to_partner(1).start()
    g.finish()
    for kind in range(4):
        for i in range(3):
            to_peers(kind, i).wait_send()
    for kind in range(3):
        pushed(kind)
    to_partner(0).wait()
    to_partner(1).wait()


def self_backward(
    ndp, pick, g, roww, colw, ca, cb, ra, rb, q, k, v, att, lse, n1g, rank, x, gain, gf, text, dk, dv, grads
):
    lp, d = g.shape
    n, lw = q.shape
    valid = x.shape[0]
    tr = text.shape[0]
    rk, slots = cb.shape[2], cb.shape[1]
    he, hl = 4 * rk, 2 * rk
    sds = jax.ShapeDtypeStruct
    nsem = 1 + 2 * (lp // SUB)
    dma = pltpu.SemaphoreType.DMA
    nb = 5 * rk + slots
    return pl.pallas_call(
        partial(self_backward_kernel, lp, ndp),
        out_shape=[
            sds((valid, d), F32),
            sds((tr // 4, d), F32),
            sds((ndp, 2 * rk, d), BF),
            sds((ndp, nb, lw), BF),
            sds((ndp, 3 * rk, lw), BF),
            sds((2, ndp, he, d), BF),
            sds((2, ndp, hl, d), BF),
        ],
        in_specs=[sspec(), vspec()] + [aspec()] * 2 + [vspec()] * 9 + [aspec()] + [vspec()] * 4 + [aspec()] + [vspec()] * 10,
        out_specs=[vspec()] * 2 + [aspec()] * 5,
        scratch_shapes=[
            VM((lp, d), F32),
            VM((n, d), BF),
            VM((n, lw), BF),
            VM((n, lw), F32),
            VM((TILE, lw), F32),
            VM((TILE, lw), F32),
            VM((n, 3 * lw), BF),
            VM((n, 128), BF),
            VM((8, n), F32),
            VM((lw, d), BF),
            VM((3 * lw, d), BF),
            VM((n, d), BF),
            VM((n, 128), BF),
            VM((n, 128), BF),
            VM((128, d), BF),
            VM((128, 3 * lw), BF),
            VM((128, lw), BF),
            VM((128, d), BF),
            VM((SUB, d), F32),
            VM((d, 2 * lw), BF),
            VM((tr, 2 * lw), BF),
            VM((tr, d), BF),
            VM((4, tr // 4, d), BF),
            VM((4, 2 * tr + 2 * rk, lw), BF),
            VM((4, 2 * tr + 2 * rk, lw), BF),
            VM((2 * he, d), BF),
            VM((4, he, d), BF),
            VM((2 * hl, d), BF),
            VM((4, hl, d), BF),
            VM((2 * rk, d), BF),
            VM((nb, lw), BF),
            VM((3 * rk, lw), BF),
            VM((he, d), BF),
            VM((hl, d), BF),
            dma((8,)),
            dma((nsem,)),
            dma((nsem,)),
            dma((4, 3)),
            dma((4, 3)),
            dma((5, ndp)),
            dma((5, ndp)),
            dma((5,)),
            dma((2,)),
            dma((2,)),
        ]
        + scatter_scratch(lp, d),
        compiler_params=params(2, 63),
        cost_estimate=cost(2 * n * d * 2560, n * d * 8),
        name="self_backward",
    )(pick, g, roww, colw, ca, cb, ra, rb, q, k, v, att, lse, n1g, rank, gain, text, x, gf, dk, dv, *grads)


def finish_kernel(
    rk, picks, ga, gb, gc, ge, gl,
    col_a, col_b, row_a, row_b, in_a, in_b, out_a, out_b,
):
    c = pl.program_id(0)
    k = picks[c]
    outs = (col_a, col_b, row_a, row_b, in_a, in_b, out_a, out_b)

    @pl.when(c == 0)
    def _():
        for o in outs:
            o[...] = jnp.zeros_like(o)

    def piece(ref, i):
        return ref[0, i * rk : i * rk + rk, :].astype(F32)

    def common(ref, i):
        per = ref.shape[2] // rk
        return ref[i // per, 0, (i % per) * rk : (i % per) * rk + rk, :].astype(F32)

    for j in range(3):
        col_a[j, k] += common(gl, j)
        col_b[j, k] += piece(gc, j)
        col_a[3 + j, k] += common(ge, j)
        col_b[3 + j, k] += piece(gb, j)
    row_b[0, k] += common(ge, 3)
    row_b[1, k] += common(ge, 4)
    in_a[k] += common(ge, 5)
    out_b[k] += common(ge, 6)
    row_a[1, k] += piece(gb, 3)
    row_a[0, k] += piece(gb, 4)
    in_b[k] += piece(ga, 0)
    out_a[k] += piece(ga, 1)


def finish(picks, ga, gb, gc, ge, gl, slots, rk, f):
    ndp, _, d = ga.shape
    lw = gb.shape[2]
    sds = jax.ShapeDtypeStruct
    shapes = [
        (6, slots, rk, d), (6, slots, rk, lw), (2, slots, rk, lw), (2, slots, rk, d),
        (slots, rk, d), (slots, rk, f), (slots, rk, f), (slots, rk, d),
    ]

    def one(x):
        return pl.BlockSpec((1,) + x.shape[1:], lambda c, p: (c, 0, 0))

    def two(x):
        return pl.BlockSpec((2, 1) + x.shape[2:], lambda c, p: (0, c, 0, 0))

    def whole(s):
        return pl.BlockSpec(s, lambda c, p: (0,) * len(s))

    return pl.pallas_call(
        partial(finish_kernel, rk),
        out_shape=[sds(s, F32) for s in shapes],
        grid_spec=pltpu.PrefetchScalarGridSpec(
            num_scalar_prefetch=1,
            grid=(ndp,),
            in_specs=[one(ga), one(gb), one(gc), two(ge), two(gl)],
            out_specs=[whole(s) for s in shapes],
        ),
        compiler_params=pltpu.CompilerParams(vmem_limit_bytes=60 * 2**20),
        cost_estimate=cost(1e6, 2e7),
        name="finish",
    )(picks, ga, gb, gc, ge, gl)


def local(
    frames_in,
    text_states,
    adapter_pick,
    out_grad,
    norm_gain,
    norm_bias,
    col_w,
    col_a,
    col_b,
    row_w,
    row_a,
    row_b,
    mlp_in,
    mlp_in_a,
    mlp_in_b,
    mlp_out,
    mlp_out_a,
    mlp_out_b,
):
    k = adapter_pick[0]
    nt_ = lax.axis_size("tensor")
    ndp = lax.axis_size("dp")
    slots = col_a.shape[1]
    valid, d = frames_in.shape
    lw = col_w.shape[2]
    rank = col_b.shape[2]
    tr = text_states.shape[0]
    cola = jnp.swapaxes(col_a, 2, 3)
    rowa = jnp.swapaxes(row_a, 2, 3)
    ia_all, oa_all = jnp.swapaxes(mlp_in_a, 1, 2), jnp.swapaxes(mlp_out_a, 1, 2)

    share = min(ndp, 8)
    piece = d // share
    part = lax.rem(lax.axis_index("dp"), share)
    stacked = jnp.swapaxes(row_w[1].reshape(lw, nt_, lw), 0, 1).reshape(d, lw)
    mine = jnp.concatenate(
        [lax.dynamic_slice_in_dim(col_w[3], part * piece, piece, 0), lax.dynamic_slice_in_dim(stacked, part * piece, piece, 0)],
        axis=0,
    )
    mine = lax.ppermute(mine, "tensor", [(i, (i + nt_ // 2) % nt_) for i in range(nt_)])
    groups = [[g * share + i for i in range(share)] for g in range(ndp // share)]
    got = lax.all_gather(mine, "dp", axis=0, tiled=False, axis_index_groups=groups)

    out0, q, kk, v, att, lse, ranks, n1g, small, ca = self_forward(
        adapter_pick, frames_in, norm_gain, norm_bias, text_states, col_w, cola, col_b, row_w, rowa, row_b
    )
    first, n2, cq, cm, second, n3, wc, wr = cross_forward(
        tr, rank, adapter_pick, out0, frames_in, norm_gain, norm_bias, col_w, row_w, got, small, ca, row_b
    )
    gn3, out3, iag, ibg, oag, obg, og_own = mlp(
        adapter_pick, n3, out_grad, mlp_in, mlp_out, ia_all, mlp_in_b, oa_all, mlp_out_b
    )
    gf, gb, dck, dcv, a3g, b3g, a1g, b1g, block_out = cross_backward(
        valid, tr, rank, adapter_pick, gn3, out3, og_own, second, first, n2, cq, cm, norm_gain, wc, wr, small, ca, row_b
    )
    frames_grad, text_grad, got_a, got_b, got_c, got_e, got_l = self_backward(
        ndp, adapter_pick, gb, row_w, col_w, ca, col_b, rowa, row_b, q, kk, v, att, lse, n1g, ranks,
        frames_in, norm_gain, gf, text_states, dck, dcv, (a3g, b3g, a1g, b1g, iag, ibg, oag, obg)
    )
    hot = got_b[:, 5 * rank :, 0].astype(F32)
    picks = jnp.sum(hot * lax.iota(F32, slots)[None, :], axis=1).astype(jnp.int32)
    col_a_grad, col_b_grad, row_a_grad, row_b_grad, in_a, in_b, out_a, out_b = finish(
        picks, got_a, got_b, got_c, got_e, got_l, slots, rank, mlp_in.shape[1]
    )
    col_a_grad = jnp.swapaxes(col_a_grad, 2, 3)
    row_a_grad = jnp.swapaxes(row_a_grad, 2, 3)
    mlp_in_a_grad, mlp_in_b_grad = jnp.swapaxes(in_a, 1, 2), in_b
    mlp_out_a_grad, mlp_out_b_grad = jnp.swapaxes(out_a, 1, 2), out_b
    return (
        block_out,
        frames_grad,
        text_grad,
        col_a_grad,
        col_b_grad,
        row_a_grad,
        row_b_grad,
        mlp_in_a_grad,
        mlp_in_b_grad,
        mlp_out_a_grad,
        mlp_out_b_grad,
    )


def solution(mesh):
    return jax.shard_map(
        local,
        mesh=mesh,
        in_specs=(
            P(("dp", "tensor"), None),
            P("dp", None),
            P("dp"),
            P("dp", None),
            P(),
            P(),
            P(None, None, "tensor"),
            P(),
            P(None, None, None, "tensor"),
            P(None, "tensor", None),
            P(None, None, "tensor", None),
            P(),
            P(None, "tensor"),
            P(),
            P(None, None, "tensor"),
            P("tensor", None),
            P(None, "tensor", None),
            P(),
        ),
        out_specs=(
            P(("dp", "tensor"), None),
            P(("dp", "tensor"), None),
            P(("dp", "tensor"), None),
            P(),
            P(None, None, None, "tensor"),
            P(None, None, "tensor", None),
            P(),
            P(),
            P(None, None, "tensor"),
            P(None, "tensor", None),
            P(),
        ),
        check_vma=False,
    )
```
